32 devices in a mesh: dp: 8 (over y, x, core), space: 4 (over z).
Axes of the slice: x: 2, y: 2, z: 4, core: 2. Of those that a mesh axis runs over, the one named last changes fastest.
Arguments:
- act_in: bfloat16 [8, 8, 64, 2048], P('dp', 'space'), may hold values from -6 to 6
- weight_one: bfloat16 [3, 3, 3, 32, 64], replicated, may hold values from -0.21875 to 0.21875
- bias_one: float32 [64], replicated, may hold values from -3 to 3
- weight_two: bfloat16 [3, 3, 3, 64, 128], replicated, may hold values from -0.15625 to 0.15625
- bias_two: float32 [128], replicated, may hold values from -3 to 3
- cotangent: bfloat16 [8, 4, 32, 4096], P('dp', 'space'), may hold values from -24 to 24
Outputs:
- grad_input: bfloat16 [8, 8, 64, 2048], P('dp', 'space')
- grad_w_one: float32 [3, 3, 3, 32, 64], replicated
- grad_b_one: float32 [64], replicated
- grad_w_two: float32 [3, 3, 3, 64, 128], replicated
- grad_b_two: float32 [128], replicated
The draws below stay inside these ranges and needn't reach their ends.
All inputs are finite; a program needn't handle non-finite values.
Results may differ from the reference program's by a relative error of at most 0.01.
Values may be sent and summed in bfloat16 or wider, within the bound.
A program may use at most 128 MiB of HBM per device.

```python
import math
import jax
import jax.numpy as jnp
from jax import lax

C0 = 32
C1 = 64
C2 = 128
SIDE = 64
BATCH = 8
DEPTH = 8
DEPTH2 = 4
HALF = 32


def levels(rng, shape, shards, smallest, high):
    gain = 1.0
    for dim, blocks in shards:
        draws = jax.random.uniform(jax.random.fold_in(jax.random.fold_in(rng, 6), dim), (blocks,), jnp.float32, smallest / len(shards), high / len(shards))
        gain = gain * jnp.repeat(jnp.exp(draws), shape[dim] // blocks).reshape((-1,) + (1,) * (len(shape) - 1 - dim))
    return gain


def centred(stream_key, dims, deviation, reach, cuts=(), kind=jnp.bfloat16):
    gain = levels(stream_key, dims, cuts, -0.22, 0.18) if cuts else 1.0
    drawn = jax.random.normal(stream_key, dims, jnp.float32) * deviation * gain
    return jnp.minimum(jnp.maximum(drawn, -reach), reach).astype(kind)


def setup_inputs(seed: int = 0) -> dict:
    splits = jax.random.split(jax.random.key(seed), 7)
    return {
        "act_in": centred(splits[0], (BATCH, DEPTH, SIDE, SIDE * C0), 1.0, 6.0, ((0, 8), (1, 4))),
        "weight_one": centred(splits[1], (3, 3, 3, C0, C1), (27 * C0) ** -0.5, 0.21875),
        "bias_one": centred(splits[2], (C1,), 0.5, 3.0, (), jnp.float32),
        "weight_two": centred(splits[3], (3, 3, 3, C1, C2), (27 * C1) ** -0.5, 0.15625),
        "bias_two": centred(splits[4], (C2,), 0.5, 3.0, (), jnp.float32),
        "cotangent": centred(splits[5], (BATCH, DEPTH2, HALF, HALF * C2), 4.0, 24.0, ((0, 8), (1, 4))),
    }


def forward_conv(padded, kernel):
    return lax.conv_general_dilated(padded, kernel, (1, 1, 1), ((0, 0), (1, 1), (1, 1)), dimension_numbers=('NDHWC', 'DHWIO', 'NDHWC'), preferred_element_type=jnp.float32)

def weight_grad(padded, delta):
    return lax.conv_general_dilated(padded, delta, (1, 1, 1), ((0, 0), (1, 1), (1, 1)), dimension_numbers=('CDHWN', 'IDHWO', 'DHWNC'), preferred_element_type=jnp.float32)

def input_grad(delta, kernel, depth_pad):
    return lax.conv_general_dilated(delta, kernel[::-1, ::-1, ::-1], (1, 1, 1), (depth_pad, (1, 1), (1, 1)), dimension_numbers=('NDHWC', 'DHWOI', 'NDHWC'), preferred_element_type=jnp.float32)

def silu_slope(value):
    sig = jax.nn.sigmoid(value)
    return sig * (1.0 + value * (1.0 - sig))

def reference(act_in, weight_one, bias_one, weight_two, bias_two, cotangent):

    def single(pair):
        sample, cot = pair
        x_five = sample.reshape(1, DEPTH, SIDE, SIDE, C0)
        x_pad = jnp.pad(x_five, ((0, 0), (1, 1), (0, 0), (0, 0), (0, 0)))
        pre_one = forward_conv(x_pad, weight_one) + bias_one
        act_one = pre_one * jax.nn.sigmoid(pre_one)
        pooled = act_one.reshape(1, DEPTH2, 2, HALF, 2, HALF, 2, C1).mean(axis=(2, 4, 6)).astype(jnp.bfloat16)
        pool_pad = jnp.pad(pooled, ((0, 0), (1, 1), (0, 0), (0, 0), (0, 0)))
        pre_two = forward_conv(pool_pad, weight_two) + bias_two
        cot_five = cot.reshape(1, DEPTH2, HALF, HALF, C2).astype(jnp.float32)
        delta_two = (cot_five * silu_slope(pre_two)).astype(jnp.bfloat16)
        gw_two = weight_grad(pool_pad, delta_two)
        gb_two = lax.optimization_barrier(jnp.sum(delta_two, axis=(0, 1, 2, 3), dtype=jnp.float32))
        grad_pooled = input_grad(delta_two, weight_two, (1, 1))
        spread = jnp.broadcast_to(grad_pooled[:, :, None, :, None, :, None, :], (1, DEPTH2, 2, HALF, 2, HALF, 2, C1)).reshape(1, DEPTH, SIDE, SIDE, C1)
        delta_one = (spread / 8.0 * silu_slope(pre_one)).astype(jnp.bfloat16)
        gw_one = weight_grad(x_pad, delta_one)
        gb_one = lax.optimization_barrier(jnp.sum(delta_one, axis=(0, 1, 2, 3), dtype=jnp.float32))
        grad_x = input_grad(delta_one, weight_one, (1, 1)).astype(jnp.bfloat16).reshape(DEPTH, SIDE, SIDE * C0)
        return (grad_x, gw_one, gb_one, gw_two, gb_two)
    grad_x, gw_one, gb_one, gw_two, gb_two = lax.map(single, (act_in, cotangent))
    scale_one = 16.0 / math.sqrt(BATCH * DEPTH * SIDE * SIDE)
    scale_two = 1.0 / math.sqrt(BATCH * DEPTH2 * HALF * HALF)
    return (grad_x, lax.optimization_barrier(jnp.sum(gw_one, axis=0)) * scale_one, lax.optimization_barrier(jnp.sum(gb_one, axis=0)) * scale_one, lax.optimization_barrier(jnp.sum(gw_two, axis=0)) * scale_two, lax.optimization_barrier(jnp.sum(gb_two, axis=0)) * scale_two)
```

```python
import functools
import math

import jax
import jax.numpy as jnp
from jax import lax
from jax.experimental import pallas as pl
from jax.experimental.pallas import tpu as pltpu
from jax.sharding import PartitionSpec as P

MESH = pl.DeviceIdType.MESH


def padded(cells, axis):
    count = lax.axis_size(axis)
    ends = count - 1
    head = cells[:, :1]
    tail = cells[:, -1:]
    before = lax.ppermute(tail, axis, [(i, (i + 1) % count) for i in range(ends)])
    after = lax.ppermute(head, axis, [((i + 1) % count, i) for i in range(ends)])
    return jnp.concatenate([before, cells, after], axis=1)


def grouped_kernel(kernel, group):
    k, j, i, c, o = kernel.shape
    parts = [
        jnp.pad(kernel, ((0, 0), (0, 0), (group - 1 + w, 2 * group - 2 - w), (0, 0), (0, 0)))
        for w in range(group)
    ]
    return jnp.concatenate(parts, axis=4).reshape(k, j, 3, group * c, group * o)


def ungrouped_grad(grad, group):
    k, j, i, cc, oo = grad.shape
    c, o = cc // group, oo // group
    cells = grad.reshape(k, j, 3 * group, c, oo)
    total = None
    for w in range(group):
        part = cells[:, :, group - 1 + w : group + 2 + w, :, w * o : (w + 1) * o]
        total = part if total is None else total + part
    return total


def forward_conv(cells, kernel):
    return lax.conv_general_dilated(
        cells,
        kernel,
        (1, 1, 1),
        ((0, 0), (1, 1), (1, 1)),
        dimension_numbers=("NDHWC", "DHWIO", "NDHWC"),
        preferred_element_type=jnp.float32,
    )


def weight_grad(cells, delta):
    return lax.conv_general_dilated(
        cells,
        delta,
        (1, 1, 1),
        ((0, 0), (1, 1), (1, 1)),
        dimension_numbers=("CDHWN", "IDHWO", "DHWNC"),
        preferred_element_type=jnp.float32,
    )


def input_grad(delta, kernel):
    return lax.conv_general_dilated(
        delta,
        kernel[::-1, ::-1, ::-1],
        (1, 1, 1),
        ((0, 0), (1, 1), (1, 1)),
        dimension_numbers=("NDHWC", "DHWOI", "NDHWC"),
        preferred_element_type=jnp.float32,
    )


def silu_slope(value):
    sig = jax.nn.sigmoid(value)
    return sig * (1.0 + value * (1.0 - sig))


def sum_kernel(n, m, x_ref, out_ref, got_dp, acc, part, got_space, send, recv, send_s, recv_s):
    me = lax.axis_index("dp")
    my = lax.axis_index("space")

    def to_dp(k, src, dst, base):
        return pltpu.make_async_remote_copy(
            src_ref=src,
            dst_ref=dst,
            send_sem=send.at[base + k],
            recv_sem=recv.at[base + k],
            device_id=(lax.rem(me + k, n), my),
            device_id_type=MESH,
        )

    def to_space(k, src, dst, base):
        return pltpu.make_async_remote_copy(
            src_ref=src,
            dst_ref=dst,
            send_sem=send_s.at[base + k],
            recv_sem=recv_s.at[base + k],
            device_id=(me, lax.rem(my + k, m)),
            device_id_type=MESH,
        )

    barrier = pltpu.get_barrier_semaphore()
    for k in range(1, n):
        pl.semaphore_signal(barrier, inc=1, device_id=(lax.rem(me + k, n), my), device_id_type=MESH)
    for k in range(1, m):
        pl.semaphore_signal(barrier, inc=1, device_id=(me, lax.rem(my + k, m)), device_id_type=MESH)
    pl.semaphore_wait(barrier, n + m - 2)

    copies = [to_dp(k, x_ref.at[lax.rem(me + k, n)], got_dp.at[k], 0) for k in range(1, n)]
    for copy in copies:
        copy.start()
    acc[...] = x_ref[me].astype(jnp.float32)
    for k, copy in enumerate(copies):
        copy.wait_recv()
        acc[...] += got_dp[k + 1].astype(jnp.float32)
    for copy in copies:
        copy.wait_send()

    part[...] = acc[...].astype(part.dtype)
    copies = [to_space(k, part.at[lax.rem(my + k, m)], got_space.at[k], 0) for k in range(1, m)]
    for copy in copies:
        copy.start()
    total = acc[my]
    for k, copy in enumerate(copies):
        copy.wait_recv()
        total = total + got_space[k + 1].astype(jnp.float32)
    for copy in copies:
        copy.wait_send()
    out_ref[me, my] = total.astype(out_ref.dtype)

    copies = [to_space(k, out_ref.at[me, my], out_ref.at[me, my], m) for k in range(1, m)]
    for copy in copies:
        copy.start()
    for copy in copies:
        copy.wait_recv()
    for copy in copies:
        copy.wait_send()

    copies = [to_dp(k, out_ref.at[me], out_ref.at[me], n) for k in range(1, n)]
    for copy in copies:
        copy.start()
    for copy in copies:
        copy.wait_recv()
    for copy in copies:
        copy.wait_send()


def summed(rows, n, m):
    count = rows.shape[0]
    each = -(-count // (n * m))
    x = jnp.pad(rows, ((0, n * m * each - count), (0, 0))).reshape(n, m, each, 128)
    out = pl.pallas_call(
        functools.partial(sum_kernel, n, m),
        out_shape=jax.ShapeDtypeStruct(x.shape, x.dtype),
        in_specs=[pl.BlockSpec(memory_space=pltpu.VMEM)],
        out_specs=pl.BlockSpec(memory_space=pltpu.VMEM),
        scratch_shapes=[
            pltpu.VMEM((n, m, each, 128), x.dtype),
            pltpu.VMEM((m, each, 128), jnp.float32),
            pltpu.VMEM((m, each, 128), x.dtype),
            pltpu.VMEM((m, each, 128), x.dtype),
            pltpu.SemaphoreType.DMA((2 * n,)),
            pltpu.SemaphoreType.DMA((2 * n,)),
            pltpu.SemaphoreType.DMA((2 * m,)),
            pltpu.SemaphoreType.DMA((2 * m,)),
        ],
        compiler_params=pltpu.CompilerParams(collective_id=0, has_side_effects=True),
    )(x)
    return out.reshape(-1, 128)[:count]


def to_rows(array):
    flat = array.reshape(-1)
    short = -flat.shape[0] % 128
    return jnp.pad(flat, (0, short)).reshape(-1, 128).astype(jnp.bfloat16)


def local(n, m, act_in, weight_one, bias_one, weight_two, bias_two, cotangent):
    samples, slab, side, merged = act_in.shape
    chan_in = weight_one.shape[3]
    chan_mid = weight_one.shape[4]
    chan_out = weight_two.shape[4]
    half = side // 2
    slab_two = slab // 2
    batch_all = samples * n
    depth_all = slab * m
    scale_one = 16.0 / math.sqrt(batch_all * depth_all * side * side)
    scale_two = 1.0 / math.sqrt(batch_all * (depth_all // 2) * half * half)
    group = max(2, 128 // chan_in)
    pair = group // 2
    wide = side // group

    kernel_one = grouped_kernel(weight_one, group)
    kernel_two = grouped_kernel(weight_two, pair)

    x_pad = padded(act_in, "space").reshape(samples, slab + 2, side, wide, group * chan_in)
    pre_one = forward_conv(x_pad, kernel_one) + jnp.tile(bias_one, group)
    act_one = pre_one * jax.nn.sigmoid(pre_one)
    quad = act_one.reshape(samples, slab_two, 2, half, 2, wide, group * chan_mid).sum(axis=(2, 4))
    pooled = jnp.concatenate(
        [
            quad[..., 2 * p * chan_mid : (2 * p + 1) * chan_mid]
            + quad[..., (2 * p + 1) * chan_mid : (2 * p + 2) * chan_mid]
            for p in range(pair)
        ],
        axis=-1,
    )
    pooled = (pooled * 0.125).astype(jnp.bfloat16)
    pool_pad = padded(pooled, "space")
    pre_two = forward_conv(pool_pad, kernel_two) + jnp.tile(bias_two, pair)
    cot = cotangent.reshape(samples, slab_two, half, wide, pair * chan_out)
    delta_two = (cot.astype(jnp.float32) * silu_slope(pre_two)).astype(jnp.bfloat16)
    delta_two_pad = padded(delta_two, "space")
    gw_two = ungrouped_grad(weight_grad(pool_pad, delta_two), pair)
    gb_two = jnp.sum(delta_two, axis=(0, 1, 2, 3), dtype=jnp.float32).reshape(pair, chan_out).sum(0)
    grad_pooled = input_grad(delta_two_pad, kernel_two) * 0.125
    spread = jnp.concatenate(
        [
            grad_pooled[..., (p // 2) * chan_mid : (p // 2 + 1) * chan_mid]
            for p in range(group)
        ],
        axis=-1,
    )
    spread = jnp.broadcast_to(
        spread[:, :, None, :, None], (samples, slab_two, 2, half, 2, wide, group * chan_mid)
    ).reshape(pre_one.shape)
    delta_one = (spread * silu_slope(pre_one)).astype(jnp.bfloat16)
    delta_one_pad = padded(delta_one, "space")
    gw_one = ungrouped_grad(weight_grad(x_pad, delta_one), group)
    gb_one = jnp.sum(delta_one, axis=(0, 1, 2, 3), dtype=jnp.float32).reshape(group, chan_mid).sum(0)
    grads = ((gw_one, scale_one), (gb_one, scale_one), (gw_two, scale_two), (gb_two, scale_two))
    order = (2, 0, 1, 3)
    rows = [to_rows(grads[i][0]) for i in order]
    stacked, delta_one_pad = lax.optimization_barrier((jnp.concatenate(rows, axis=0), delta_one_pad))
    total = summed(stacked, n, m)
    grad_x = input_grad(delta_one_pad, kernel_one)
    grad_input = grad_x.astype(jnp.bfloat16).reshape(samples, slab, side, side * chan_in)
    outs = {}
    start = 0
    for i, block in zip(order, rows):
        grad, scale = grads[i]
        own = total[start : start + block.shape[0]].astype(jnp.float32) * scale
        outs[i] = own.reshape(-1)[: grad.size].reshape(grad.shape)
        start += block.shape[0]
    return grad_input, outs[0], outs[1], outs[2], outs[3]


def solution(mesh):
    placed = (P("dp", "space", None, None), P(), P(), P(), P(), P("dp", "space", None, None))
    return jax.shard_map(
        functools.partial(local, mesh.shape["dp"], mesh.shape["space"]),
        mesh=mesh,
        in_specs=placed,
        out_specs=(P("dp", "space", None, None), P(), P(), P(), P()),
        check_vma=False,
    )
```
